32 devices in a mesh: occ: 4 (over y, core), aux: 8 (over z, x).
Axes of the slice: x: 2, y: 2, z: 4, core: 2. Of those that a mesh axis runs over, the one named last changes fastest.
Arguments:
- pair_ints: bfloat16 [16, 128, 20480], P(None, None, ('aux', 'occ')), may hold values from -110 to 110
- domain_len: int32 [4], replicated, may hold values from 1 to 4, as said below
- domain_blocks: int32 [4, 4], replicated, may hold values from 0 to 703
- slot_orbital: int32 [4], replicated, may hold values from 0 to 3, each once
- virt_energy: float32 [90112], replicated, may hold values from 0.1 to 3
- occ_energy: float32 [4], replicated, may hold values from -2 to -0.3
Outputs:
- projected: bfloat16 [4, 512, 20480], P('occ', None, 'aux')
The draws below stay inside these ranges and needn't reach their ends.
Inputs may be any that keep to these rules, and one draw needn't show every extreme that they name: `domain_len`: some orbital has exactly 4 live blocks. `slot_orbital`: each orbital is owned by exactly one group.
All inputs are finite; a program needn't handle non-finite values.
Results may differ from the reference program's by a relative error of at most 0.001.
The reference program's roundings to bfloat16 on the way count: a program that leaves them out, or rounds other values in their place, can miss the bound.
Values may be sent and summed in bfloat16 or wider, within the bound.
A program may use at most 128 MiB of HBM per device.

```python
import math
import jax
import jax.numpy as jnp
from jax import lax

VB = 128
DOM_BLK = 4
NVB = 704
DOM = 512
NVIRT = 90112
NAUX = 20480
NORB = 4
NBLK = 16


def draw_pair_ints(key, part):
    noise_key, row_key, col_key = jax.random.split(key, 3)
    column = jnp.arange(NAUX, dtype=jnp.float32) / NAUX
    coupling = 0.1 + 0.8 * column
    noise_draw = jnp.clip(jax.random.normal(noise_key, (NBLK, VB, NAUX), jnp.float32), -6.0, 6.0)
    row_scale = jnp.exp(jax.random.uniform(row_key, (NBLK, VB, 1), jnp.float32, math.log(0.3), math.log(3.0)))
    col_groups = jnp.exp(jax.random.uniform(col_key, (NBLK, 1, NAUX // 64), jnp.float32, math.log(0.3), math.log(3.0)))
    col_scale = jnp.repeat(col_groups, 64, axis=2)
    neighbor = jnp.roll(noise_draw, -1, axis=1)
    values = (noise_draw + coupling * neighbor) * row_scale * col_scale / jnp.sqrt(1.0 + coupling * coupling)
    return values.astype(jnp.bfloat16)


def draw_domain_len(key, part):
    value_key, place_key = jax.random.split(jax.random.fold_in(key, 17), 2)
    values = jax.random.randint(value_key, (NORB,), 1, DOM_BLK + 1, dtype=jnp.int32)
    place = jax.random.randint(place_key, (), 0, NORB, dtype=jnp.int32)
    return jnp.where(jnp.arange(NORB, dtype=jnp.int32) == place, DOM_BLK, values).astype(jnp.int32)


def plant(values, own_key, least, top_value):
    extent = values.shape
    spot = [jax.random.randint(jax.random.fold_in(own_key, axis), (), 0, extent[axis]) for axis in range(len(extent))]
    values = values.at[tuple(spot)].set(least)
    longest = extent.index(max(extent))
    spot[longest] = (spot[longest] + 1) % extent[longest]
    return values.at[tuple(spot)].set(top_value)


def setup_inputs(seed: int = 0) -> dict:
    streams_of = jax.random.split(jax.random.key(seed), 7)
    return {
        "pair_ints": draw_pair_ints(jax.random.fold_in(streams_of[6], 71), 0),
        "domain_len": draw_domain_len(jax.random.fold_in(streams_of[6], 71), 0),
        "domain_blocks": plant(jax.random.randint(streams_of[2], (NORB, DOM_BLK), 0, NVB), jax.random.fold_in(streams_of[2], 1), 0, NVB - 1).astype(jnp.int32),
        "slot_orbital": jax.random.permutation(streams_of[3], NORB).astype(jnp.int32),
        "virt_energy": jnp.clip(jax.random.uniform(streams_of[4], (NVIRT,), jnp.float32, 0.1, 3.0), 0.1, 3.0),
        "occ_energy": jnp.clip(jax.random.uniform(streams_of[5], (NORB,), jnp.float32, -2.0, -0.3), -2.0, -0.3),
    }


LEVEL_RATIO = 0.5
EPSILON = 1e-05

def reference(pair_ints, domain_len, domain_blocks, slot_orbital, virt_energy, occ_energy):
    slot_ids = jnp.arange(DOM_BLK, dtype=jnp.int32)
    energy_table = virt_energy.reshape(NVB, VB)

    def project_one(orbital):
        length = domain_len[orbital]
        live_mask = slot_ids < length
        block_index = (orbital * DOM_BLK + slot_ids).astype(jnp.int32)
        picked = jnp.take(pair_ints, block_index, axis=0)
        picked = jnp.where(live_mask[:, None, None], picked, jnp.zeros_like(picked))
        domain_rows = picked.reshape(DOM, NAUX).astype(jnp.float32)
        gram_sum = jnp.dot(domain_rows, domain_rows.T, precision=lax.Precision.HIGHEST)
        energies = jnp.take(energy_table, domain_blocks[orbital], axis=0).reshape(DOM)
        denominator = energies[:, None] + energies[None, :] - 2.0 * occ_energy[orbital]
        amplitude = gram_sum / denominator
        level_shift = LEVEL_RATIO * (jnp.trace(amplitude) / (VB * length.astype(jnp.float32)) + EPSILON)
        factor = jnp.linalg.cholesky(amplitude + level_shift * jnp.eye(DOM, dtype=jnp.float32))
        solved = jax.scipy.linalg.cho_solve((factor, True), amplitude)
        projector = lax.optimization_barrier(solved.T.astype(jnp.bfloat16)).astype(jnp.float32)
        return jnp.dot(projector, domain_rows, precision=lax.Precision.HIGHEST).astype(jnp.bfloat16)
    return lax.map(project_one, slot_orbital)
```

```python
import jax
import jax.numpy as jnp
from jax import lax
from jax.experimental import pallas as pl
from jax.experimental.pallas import tpu as pltpu
from jax.sharding import PartitionSpec as P

LEVEL_RATIO = 0.5
EPSILON = 1e-05
F32 = jnp.float32
BF16 = jnp.bfloat16


def split(value):
    high = value.astype(BF16)
    return high, (value - high.astype(F32)).astype(BF16)


def dot(a, b):
    return jnp.dot(a, b, preferred_element_type=F32)


def solve_kernel(
    scale_ref, gram_ref, col_ref, row_ref, rows_hbm, out_hbm,
    m_high, m_low, x_ref, r_ref, rows_buf, out_buf, in_sem, out_sem,
):
    size = gram_ref.shape[0]
    tiles, _, width = out_buf.shape

    def fetch(t):
        return pltpu.make_async_copy(
            rows_hbm.at[:, pl.ds(t * width, width)], rows_buf.at[t], in_sem.at[t]
        )

    def flush(t):
        return pltpu.make_async_copy(
            out_buf.at[t], out_hbm.at[:, pl.ds(t * width, width)], out_sem.at[t]
        )

    for t in range(tiles):
        fetch(t).start()

    eye = (
        lax.broadcasted_iota(jnp.int32, (size, size), 0)
        == lax.broadcasted_iota(jnp.int32, (size, size), 1)
    ).astype(F32)
    amplitude = gram_ref[...] / (col_ref[...] + row_ref[...] - 2.0 * scale_ref[0])
    trace = jnp.sum(amplitude * eye)
    level_shift = LEVEL_RATIO * (trace / scale_ref[1] + EPSILON)
    row_sum = jnp.max(jnp.sum(jnp.abs(amplitude), axis=0, keepdims=True))
    upper = level_shift + 1.01 * jnp.minimum(row_sum, 1.01 * trace)
    unit = 2.0 / (level_shift + upper)
    start = level_shift * unit
    scaled = (amplitude + level_shift * eye) * unit
    high, low = split(scaled)
    m_high[...] = high
    m_low[...] = low

    def factor(rho):
        return 2.0 / (1.0 + rho * (2.0 - rho))

    def advance(rho):
        return factor(rho) * rho * (2.0 - rho)

    x_ref[...] = factor(start) * (2.0 * eye - scaled)

    def quick(rho):
        x = x_ref[...]
        xb = x.astype(BF16)
        t = dot(m_high[...], xb)
        x_ref[...] = factor(rho) * (2.0 * x - dot(xb, t.astype(BF16)))
        return advance(rho)

    rho = lax.while_loop(lambda rho: rho < 0.95, quick, advance(start))
    del rho

    def times_m(x):
        xh, xl = split(x)
        mh = m_high[...]
        return dot(mh, xh) + (dot(mh, xl) + dot(m_low[...], xh))

    def residual():
        r = eye_again() - times_m(x_ref[...])
        r_ref[...] = r
        return jnp.sum(r * r)

    def eye_again():
        return (
            lax.broadcasted_iota(jnp.int32, (size, size), 0)
            == lax.broadcasted_iota(jnp.int32, (size, size), 1)
        ).astype(F32)

    def x_times(value):
        xh, xl = split(x_ref[...])
        vh, vl = split(value)
        return dot(xh, vh) + (dot(xh, vl) + dot(xl, vh))

    norm = residual()

    def careful(rho):
        x_ref[...] = factor(rho) * (2.0 * x_ref[...] - x_times(times_m(x_ref[...])))
        return advance(rho)

    def restart(_):
        x_ref[...] = eye_again()
        lax.while_loop(lambda rho: rho < 0.9999, careful, start)
        return residual()

    norm = lax.cond(norm < 0.9, lambda n: n, restart, norm)

    def refine(state):
        _, step = state
        x_ref[...] = x_ref[...] + x_times(r_ref[...])
        return residual(), step + 1

    lax.while_loop(
        lambda state: jnp.logical_and(state[0] > 1e-6, state[1] < 12), refine, (norm, 0)
    )
    x = x_ref[...] + x_times(r_ref[...])
    projector = (eye_again() - (level_shift * unit) * x).astype(BF16)
    m_high[...] = projector
    for t in range(tiles):
        fetch(t).wait()
        out_buf[t] = dot(m_high[...], rows_buf[t]).astype(BF16)
        flush(t).start()
    for t in range(tiles):
        flush(t).wait()


def solve_and_project(scales, gram, energies, rows):
    size, cols = rows.shape
    tiles = max(1, cols // 512)
    while cols % tiles or (cols // tiles) % 128:
        tiles -= 1
    width = cols // tiles
    vmem = pl.BlockSpec(memory_space=pltpu.VMEM)
    return pl.pallas_call(
        solve_kernel,
        out_shape=jax.ShapeDtypeStruct((size, cols), BF16),
        in_specs=[
            pl.BlockSpec(memory_space=pltpu.SMEM), vmem, vmem, vmem,
            pl.BlockSpec(memory_space=pl.ANY),
        ],
        out_specs=pl.BlockSpec(memory_space=pl.ANY),
        scratch_shapes=[
            pltpu.VMEM((size, size), BF16),
            pltpu.VMEM((size, size), BF16),
            pltpu.VMEM((size, size), F32),
            pltpu.VMEM((size, size), F32),
            pltpu.VMEM((tiles, size, width), BF16),
            pltpu.VMEM((tiles, size, width), BF16),
            pltpu.SemaphoreType.DMA((tiles,)),
            pltpu.SemaphoreType.DMA((tiles,)),
        ],
        compiler_params=pltpu.CompilerParams(vmem_limit_bytes=48 << 20),
        name="solve",
    )(scales, gram, energies[:, None], energies[None, :], rows)


def local(pair_ints, domain_len, domain_blocks, slot_orbital, virt_energy, occ_energy):
    orbitals = domain_len.shape[0]
    block_count = domain_blocks.shape[1]
    block_rows = pair_ints.shape[1]
    local_cols = pair_ints.shape[2]
    domain_size = block_count * block_rows
    slot_ids = jnp.arange(block_count, dtype=jnp.int32)
    ordered_len = jnp.take(domain_len, slot_orbital, axis=0)
    starts = (slot_orbital * block_count)[:, None] + slot_ids[None, :]
    live_mask = slot_ids[None, :] < ordered_len[:, None]
    picked = jnp.take(pair_ints, starts.reshape(-1), axis=0)
    picked = jnp.where(live_mask.reshape(-1)[:, None, None], picked, jnp.zeros_like(picked))
    padded = picked.reshape(orbitals, domain_size, local_cols)
    own_rows = lax.all_to_all(padded, "occ", split_axis=0, concat_axis=2, tiled=True)[0]
    orbital = lax.dynamic_index_in_dim(slot_orbital, lax.axis_index("occ"), 0, keepdims=False)
    gram = lax.psum(jnp.einsum("ac,bc->ab", own_rows, own_rows, preferred_element_type=F32), "aux")
    blocks = lax.dynamic_index_in_dim(domain_blocks, orbital, 0, keepdims=False)
    energies = jnp.take(virt_energy.reshape(-1, block_rows), blocks, axis=0).reshape(domain_size)
    occ_level = lax.dynamic_index_in_dim(occ_energy, orbital, 0, keepdims=False)
    length = lax.dynamic_index_in_dim(domain_len, orbital, 0, keepdims=False).astype(F32)
    scales = jnp.stack([occ_level, block_rows * length])
    return solve_and_project(scales, gram, energies, own_rows)[None]


def solution(mesh):
    placed = (P(None, None, ("aux", "occ")), P(), P(), P(), P(), P())
    return jax.shard_map(
        local, mesh=mesh, in_specs=placed, out_specs=P("occ", None, "aux"), check_vma=False
    )
```

```python
import functools

import jax
import jax.numpy as jnp
from jax import lax
from jax.experimental import pallas as pl
from jax.experimental.pallas import tpu as pltpu
from jax.sharding import PartitionSpec as P

LEVEL_RATIO = 0.5
EPSILON = 1e-05
F32 = jnp.float32
BF16 = jnp.bfloat16


def split(value):
    high = value.astype(BF16)
    return high, (value - high.astype(F32)).astype(BF16)


def dot(a, b):
    return jnp.dot(a, b, preferred_element_type=F32)


def gather_kernel(slot_ref, len_ref, pair_ref, padded_ref, packed_ref):
    blocks, size, cols = pair_ref.shape
    length = len_ref[slot_ref[pl.program_id(0)]]
    for k in range(blocks):
        rows = pair_ref[k]
        padded_ref[0, k * size:(k + 1) * size, :] = jnp.where(k < length, rows, jnp.zeros_like(rows))
    place = 0
    for i in range(blocks):
        band = lax.dot_general(
            padded_ref[0, i * size:(i + 1) * size, :],
            padded_ref[0, :(i + 1) * size, :],
            (((1,), (1,)), ((), ())),
            preferred_element_type=F32,
        )
        for j in range(i + 1):
            packed_ref[0, place * size:(place + 1) * size, :] = band[:, j * size:(j + 1) * size]
            place += 1


def gather_and_gram(slot_orbital, domain_len, pair_ints, blocks):
    groups = slot_orbital.shape[0]
    _, size, cols = pair_ints.shape
    packed = blocks * (blocks + 1) // 2 * size
    return pl.pallas_call(
        gather_kernel,
        out_shape=(
            jax.ShapeDtypeStruct((groups, blocks * size, cols), BF16),
            jax.ShapeDtypeStruct((groups, packed, size), F32),
        ),
        grid_spec=pltpu.PrefetchScalarGridSpec(
            num_scalar_prefetch=2,
            grid=(groups,),
            in_specs=[pl.BlockSpec((blocks, size, cols), lambda g, slot, _: (slot[g], 0, 0))],
            out_specs=[
                pl.BlockSpec((1, blocks * size, cols), lambda g, *_: (g, 0, 0)),
                pl.BlockSpec((1, packed, size), lambda g, *_: (g, 0, 0)),
            ],
        ),
        compiler_params=pltpu.CompilerParams(dimension_semantics=("arbitrary",)),
        name="gather",
    )(slot_orbital, domain_len, pair_ints)


MESH = pl.DeviceIdType.MESH


def exchange_kernel(
    ny, nx, nz, part_ref, rows_ref, gram_ref, own_ref,
    core_buf, y_out, y_in, x_out, x_in, z_out, z_in,
    core_ss, core_rs, y_ss, y_rs, x_ss, x_rs, z_ss, z_rs,
    gz_ss, gz_rs, gx_ss, gx_rs, row_ss, row_rs,
):
    occ, aux = lax.axis_index("occ"), lax.axis_index("aux")
    y, core = lax.div(occ, 2), lax.rem(occ, 2)
    z, x = lax.div(aux, nx), lax.rem(aux, nx)
    piece = gram_ref.shape[0] // (nx * nz)
    chunk = piece * nz
    other = 1 - core

    def at_y(d):
        return lax.rem(y + d, ny)

    def at_x(e):
        return lax.rem(x + e, nx)

    def at_z(f):
        return lax.rem(z + f, nz)

    def chunk_of(e):
        return pl.ds(pl.multiple_of(at_x(e) * chunk, 8), chunk)

    def piece_of(xx, zz):
        return pl.ds(pl.multiple_of((xx * nz + zz) * piece, 8), piece)

    def copy(src, dst, ss, rs, to_occ, to_aux):
        return pltpu.make_async_remote_copy(
            src_ref=src, dst_ref=dst, send_sem=ss, recv_sem=rs,
            device_id=(to_occ, to_aux), device_id_type=MESH,
        )

    barrier = pltpu.get_barrier_semaphore()
    peers = [(2 * y + other, aux)]
    for d in range(1, ny):
        peers += [(2 * at_y(d) + core, aux), (2 * at_y(d) + other, aux)]
    peers += [(occ, z * nx + at_x(e)) for e in range(1, nx)]
    peers += [(occ, at_z(f) * nx + x) for f in range(1, nz)]
    for peer in peers:
        pl.semaphore_signal(barrier, inc=1, device_id=peer, device_id_type=MESH)
    pl.semaphore_wait(barrier, len(peers))

    far_y = list(range(1, ny)) + [0]
    far_x = list(range(1, nx)) + [0]
    far_z = list(range(1, nz)) + [0]

    def core_copy(d, e):
        return copy(
            part_ref.at[2 * at_y(d) + other, chunk_of(e)], core_buf.at[d, chunk_of(e)],
            core_ss.at[d, e], core_rs.at[d, e], 2 * y + other, aux,
        )

    def y_copy(d, e):
        return copy(
            y_out.at[d, chunk_of(e)], y_in.at[d, chunk_of(e)],
            y_ss.at[d, e], y_rs.at[d, e], 2 * at_y(d) + core, aux,
        )

    def x_copy(e, f):
        return copy(
            x_out.at[piece_of(at_x(e), at_z(f))], x_in.at[e, pl.ds(pl.multiple_of(at_z(f) * piece, 8), piece)],
            x_ss.at[e, f], x_rs.at[e, f], occ, z * nx + at_x(e),
        )

    def z_copy(f):
        return copy(
            z_out.at[f], z_in.at[f], z_ss.at[f], z_rs.at[f], occ, at_z(f) * nx + x,
        )

    def gz_copy(f):
        mine = gram_ref.at[piece_of(x, z)]
        return copy(mine, mine, gz_ss.at[f], gz_rs.at[f], occ, at_z(f) * nx + x)

    def gz_in(f):
        theirs = gram_ref.at[piece_of(x, lax.rem(z + nz - f, nz))]
        return copy(theirs, theirs, gz_ss.at[f], gz_rs.at[f], occ, at_z(f) * nx + x)

    def gx_copy(e, f):
        part = gram_ref.at[piece_of(x, lax.rem(z + nz - f, nz))]
        return copy(part, part, gx_ss.at[e, f], gx_rs.at[e, f], occ, z * nx + at_x(e))

    def gx_in(e, f):
        part = gram_ref.at[piece_of(lax.rem(x + nx - e, nx), lax.rem(z + nz - f, nz))]
        return copy(part, part, gx_ss.at[e, f], gx_rs.at[e, f], occ, z * nx + at_x(e))

    def row_copy(d, swap):
        target = 2 * at_y(d) + (other if swap else core)
        return copy(
            rows_ref.at[target], own_ref.at[occ], row_ss.at[d, swap], row_rs.at[d, swap], target, aux
        )

    def row_in(d, swap):
        source = 2 * lax.rem(y + ny - d, ny) + (other if swap else core)
        return copy(
            rows_ref.at[source], own_ref.at[source], row_ss.at[d, swap], row_rs.at[d, swap], source, aux
        )

    row_moves = [(d, s) for d in range(1, ny) for s in (0, 1)] + [(0, 1)]

    for d in far_y:
        for e in far_x:
            core_copy(d, e).start()
    for e in far_x:
        for d in range(1, ny):
            core_copy(d, e).wait_recv()
            y_out[d, chunk_of(e), :] = part_ref[2 * at_y(d) + core, chunk_of(e), :] + core_buf[d, chunk_of(e), :]
            y_copy(d, e).start()
    for move in row_moves:
        row_copy(*move).start()
    for e in far_x:
        core_copy(0, e).wait_recv()
        for d in range(1, ny):
            y_copy(d, e).wait_recv()
        for f in far_z:
            if e:
                span = piece_of(at_x(e), at_z(f))
                total = part_ref[occ, span, :] + core_buf[0, span, :]
                for d in range(1, ny):
                    total = total + y_in[d, span, :]
                x_out[span, :] = total
                x_copy(e, f).start()
    for f in far_z:
        span = piece_of(x, at_z(f))
        total = part_ref[occ, span, :] + core_buf[0, span, :]
        for d in range(1, ny):
            total = total + y_in[d, span, :]
        for e in range(1, nx):
            x_copy(e, f).wait_recv()
            total = total + x_in[e, pl.ds(pl.multiple_of(at_z(f) * piece, 8), piece), :]
        if f:
            z_out[f] = total
            z_copy(f).start()
        else:
            z_out[0] = total
    total = z_out[0]
    for f in range(1, nz):
        z_copy(f).wait_recv()
        total = total + z_in[f]
    gram_ref[piece_of(x, z), :] = total
    for f in range(1, nz):
        gz_copy(f).start()
    for e in range(1, nx):
        gx_copy(e, 0).start()
    for f in range(1, nz):
        gz_in(f).wait_recv()
        for e in range(1, nx):
            gx_copy(e, f).start()
    for e in range(1, nx):
        for f in range(nz):
            gx_in(e, f).wait_recv()
    for move in row_moves:
        row_in(*move).wait_recv()

    for d in far_y:
        for e in far_x:
            core_copy(d, e).wait_send()
            if d:
                y_copy(d, e).wait_send()
    for f in far_z:
        for e in range(1, nx):
            x_copy(e, f).wait_send()
            gx_copy(e, f).wait_send()
        if f:
            z_copy(f).wait_send()
            gz_copy(f).wait_send()
    for move in row_moves:
        row_copy(*move).wait_send()


def exchange(packed, padded, n_aux):
    groups, height, lanes = packed.shape
    ny = groups // 2
    nx = ny if n_aux % ny == 0 else 1
    nz = n_aux // nx
    piece = height // n_aux
    dma = pltpu.SemaphoreType.DMA
    sems = [(ny, nx)] * 4 + [(nx, nz)] * 2 + [(nz,)] * 4 + [(nx, nz)] * 2 + [(ny, 2)] * 2
    return pl.pallas_call(
        functools.partial(exchange_kernel, ny, nx, nz),
        out_shape=(
            jax.ShapeDtypeStruct((height, lanes), F32),
            jax.ShapeDtypeStruct(padded.shape, BF16),
        ),
        in_specs=[pl.BlockSpec(memory_space=pltpu.VMEM), pl.BlockSpec(memory_space=pl.ANY)],
        out_specs=[pl.BlockSpec(memory_space=pltpu.VMEM), pl.BlockSpec(memory_space=pl.ANY)],
        scratch_shapes=[
            pltpu.VMEM((ny, height, lanes), F32),
            pltpu.VMEM((ny, height, lanes), F32),
            pltpu.VMEM((ny, height, lanes), F32),
            pltpu.VMEM((height, lanes), F32),
            pltpu.VMEM((nx, piece * nz, lanes), F32),
            pltpu.VMEM((nz, piece, lanes), F32),
            pltpu.VMEM((nz, piece, lanes), F32),
        ] + [dma(shape) for shape in sems],
        compiler_params=pltpu.CompilerParams(
            collective_id=0, has_side_effects=True, vmem_limit_bytes=48 << 20
        ),
        name="exchange",
    )(packed, padded)


def solve_kernel(
    slot_ref, len_ref, block_ref, occ_ref, packed_ref, energy_hbm, own_hbm, padded_hbm, out_hbm,
    m_high, m_low, x_ref, r_ref, rows_buf, out_buf, energy_buf, in_sem, out_sem, energy_sem,
):
    size = x_ref.shape[0]
    tiles, _, width = out_buf.shape
    blocks, _, side = energy_buf.shape
    me = lax.axis_index("occ")
    orbital = slot_ref[me]

    def energy(k):
        return pltpu.make_async_copy(
            energy_hbm.at[block_ref[orbital, k]], energy_buf.at[k], energy_sem.at[k]
        )

    def fetch(t):
        return pltpu.make_async_copy(own_hbm.at[t], rows_buf.at[t], in_sem.at[t])

    def fetch_mine(t):
        return pltpu.make_async_copy(padded_hbm.at[t], rows_buf.at[t], in_sem.at[t])

    def flush(t):
        return pltpu.make_async_copy(
            out_buf.at[t], out_hbm.at[:, pl.ds(t * width, width)], out_sem.at[t]
        )

    for k in range(blocks):
        energy(k).start()
    for t in range(tiles):
        @pl.when(t == me)
        def _():
            fetch_mine(t).start()

        @pl.when(t != me)
        def _():
            fetch(t).start()

    for k in range(blocks):
        energy(k).wait()
    place = 0
    for i in range(blocks):
        column = jnp.broadcast_to(energy_buf[i], (side, side)).T
        for j in range(i + 1):
            level = column + jnp.broadcast_to(energy_buf[j], (side, side)) - 2.0 * occ_ref[orbital]
            part = packed_ref[place * side:(place + 1) * side, :] / level
            x_ref[i * side:(i + 1) * side, j * side:(j + 1) * side] = part
            if j < i:
                x_ref[j * side:(j + 1) * side, i * side:(i + 1) * side] = part.T
            place += 1

    eye = (
        lax.broadcasted_iota(jnp.int32, (size, size), 0)
        == lax.broadcasted_iota(jnp.int32, (size, size), 1)
    ).astype(F32)
    amplitude = x_ref[...]
    trace = jnp.sum(amplitude * eye)
    live = (side * len_ref[orbital]).astype(F32)
    level_shift = LEVEL_RATIO * (trace / live + EPSILON)
    row_sum = jnp.max(jnp.sum(jnp.abs(amplitude), axis=0, keepdims=True))
    upper = level_shift + 1.01 * jnp.minimum(row_sum, 1.01 * trace)
    unit = 2.0 / (level_shift + upper)
    start = level_shift * unit
    scaled = (amplitude + level_shift * eye) * unit
    high, low = split(scaled)
    m_high[...] = high
    m_low[...] = low

    def factor(rho):
        return 2.0 / (1.0 + rho * (2.0 - rho))

    def advance(rho):
        return factor(rho) * rho * (2.0 - rho)

    x_ref[...] = factor(start) * (2.0 * eye - scaled)

    def quick(rho):
        x = x_ref[...]
        xb = x.astype(BF16)
        t = dot(m_high[...], xb)
        x_ref[...] = factor(rho) * (2.0 * x - dot(xb, t.astype(BF16)))
        return advance(rho)

    rho = lax.while_loop(lambda rho: rho < 0.95, quick, advance(start))
    del rho

    def times_m(x):
        xh, xl = split(x)
        mh = m_high[...]
        return dot(mh, xh) + (dot(mh, xl) + dot(m_low[...], xh))

    def residual():
        r = eye_again() - times_m(x_ref[...])
        r_ref[...] = r
        return jnp.sum(r * r)

    def eye_again():
        return (
            lax.broadcasted_iota(jnp.int32, (size, size), 0)
            == lax.broadcasted_iota(jnp.int32, (size, size), 1)
        ).astype(F32)

    def x_times(value):
        xh, xl = split(x_ref[...])
        vh, vl = split(value)
        return dot(xh, vh) + (dot(xh, vl) + dot(xl, vh))

    norm = residual()

    def careful(rho):
        x_ref[...] = factor(rho) * (2.0 * x_ref[...] - x_times(times_m(x_ref[...])))
        return advance(rho)

    def restart(_):
        x_ref[...] = eye_again()
        lax.while_loop(lambda rho: rho < 0.9999, careful, start)
        return residual()

    norm = lax.cond(norm < 0.9, lambda n: n, restart, norm)

    def refine(state):
        _, step = state
        x_ref[...] = x_ref[...] + x_times(r_ref[...])
        return residual(), step + 1

    lax.while_loop(
        lambda state: jnp.logical_and(state[0] > 1e-6, state[1] < 12), refine, (norm, 0)
    )
    x = x_ref[...] + x_times(r_ref[...])
    projector = (eye_again() - (level_shift * unit) * x).astype(BF16)
    m_high[...] = projector
    for t in range(tiles):
        fetch(t).wait()
        out_buf[t] = dot(m_high[...], rows_buf[t]).astype(BF16)
        flush(t).start()
    for t in range(tiles):
        flush(t).wait()


def solve_and_project(slot_orbital, domain_len, domain_blocks, occ_energy, packed, table, own, padded):
    groups, size, width = own.shape
    blocks = domain_blocks.shape[1]
    side = size // blocks
    vmem = pl.BlockSpec(memory_space=pltpu.VMEM)
    smem = pl.BlockSpec(memory_space=pltpu.SMEM)
    hbm = pl.BlockSpec(memory_space=pl.ANY)
    return pl.pallas_call(
        solve_kernel,
        out_shape=jax.ShapeDtypeStruct((size, groups * width), BF16),
        in_specs=[smem] * 4 + [vmem] + [hbm] * 3,
        out_specs=hbm,
        scratch_shapes=[
            pltpu.VMEM((size, size), BF16),
            pltpu.VMEM((size, size), BF16),
            pltpu.VMEM((size, size), F32),
            pltpu.VMEM((size, size), F32),
            pltpu.VMEM((groups, size, width), BF16),
            pltpu.VMEM((groups, size, width), BF16),
            pltpu.VMEM((blocks, 1, side), F32),
            pltpu.SemaphoreType.DMA((groups,)),
            pltpu.SemaphoreType.DMA((groups,)),
            pltpu.SemaphoreType.DMA((blocks,)),
        ],
        compiler_params=pltpu.CompilerParams(vmem_limit_bytes=48 << 20),
        name="solve",
    )(slot_orbital, domain_len, domain_blocks, occ_energy, packed, table, own, padded)


def solution(mesh):
    n_aux = mesh.shape["aux"]

    def local(pair_ints, domain_len, domain_blocks, slot_orbital, virt_energy, occ_energy):
        blocks = domain_blocks.shape[1]
        padded, packed = gather_and_gram(slot_orbital, domain_len, pair_ints, blocks)
        gram, own = exchange(packed, padded, n_aux)
        table = virt_energy.reshape(-1, 1, pair_ints.shape[1])
        return solve_and_project(
            slot_orbital, domain_len, domain_blocks, occ_energy, gram, table, own, padded
        )[None]

    placed = (P(None, None, ("aux", "occ")), P(), P(), P(), P(), P())
    return jax.shard_map(
        local, mesh=mesh, in_specs=placed, out_specs=P("occ", None, "aux"), check_vma=False
    )
```

```python
import functools

import jax
import jax.numpy as jnp
from jax import lax
from jax.experimental import pallas as pl
from jax.experimental.pallas import tpu as pltpu
from jax.sharding import PartitionSpec as P

LEVEL_RATIO = 0.5
EPSILON = 1e-05
F32 = jnp.float32
BF16 = jnp.bfloat16


def split(value):
    high = value.astype(BF16)
    return high, (value - high.astype(F32)).astype(BF16)


def dot(a, b):
    return jnp.dot(a, b, preferred_element_type=F32)


MESH = pl.DeviceIdType.MESH


def exchange_kernel(
    ny, nx, nz, slot_ref, len_ref, pair_hbm, gram_ref, own_ref,
    pair_buf, pad_buf, part_ref, core_buf, y_out, y_in, x_out, x_in, z_out, z_in,
    core_ss, core_rs, y_ss, y_rs, x_ss, x_rs, z_ss, z_rs,
    gz_ss, gz_rs, gx_ss, gx_rs, row_ss, row_rs, pair_sem, mine_sem,
):
    occ, aux = lax.axis_index("occ"), lax.axis_index("aux")
    y, core = lax.div(occ, 2), lax.rem(occ, 2)
    z, x = lax.div(aux, nx), lax.rem(aux, nx)
    piece = gram_ref.shape[0] // (nx * nz)
    chunk = piece * nz
    other = 1 - core

    def at_y(d):
        return lax.rem(y + d, ny)

    def at_x(e):
        return lax.rem(x + e, nx)

    def at_z(f):
        return lax.rem(z + f, nz)

    def chunk_of(e):
        return pl.ds(pl.multiple_of(at_x(e) * chunk, 8), chunk)

    def piece_of(xx, zz):
        return pl.ds(pl.multiple_of((xx * nz + zz) * piece, 8), piece)

    def copy(src, dst, ss, rs, to_occ, to_aux):
        return pltpu.make_async_remote_copy(
            src_ref=src, dst_ref=dst, send_sem=ss, recv_sem=rs,
            device_id=(to_occ, to_aux), device_id_type=MESH,
        )

    groups, domain, _ = pad_buf.shape
    size = pair_buf.shape[1]
    blocks = domain // size

    def load(g):
        span = pl.ds(g * blocks, blocks)
        return pltpu.make_async_copy(pair_hbm.at[span], pair_buf.at[span], pair_sem.at[g])

    for g in range(groups):
        load(g).start()
    barrier = pltpu.get_barrier_semaphore()
    peers = [(2 * y + other, aux)]
    for d in range(1, ny):
        peers += [(2 * at_y(d) + core, aux), (2 * at_y(d) + other, aux)]
    peers += [(occ, z * nx + at_x(e)) for e in range(1, nx)]
    peers += [(occ, at_z(f) * nx + x) for f in range(1, nz)]
    for peer in peers:
        pl.semaphore_signal(barrier, inc=1, device_id=peer, device_id_type=MESH)
    pl.semaphore_wait(barrier, len(peers))

    far_y = list(range(1, ny)) + [0]
    far_x = list(range(1, nx)) + [0]
    far_z = list(range(1, nz)) + [0]

    def core_copy(d, e):
        return copy(
            part_ref.at[2 * at_y(d) + other, chunk_of(e)], core_buf.at[d, chunk_of(e)],
            core_ss.at[d, e], core_rs.at[d, e], 2 * y + other, aux,
        )

    def y_copy(d, e):
        return copy(
            y_out.at[d, chunk_of(e)], y_in.at[d, chunk_of(e)],
            y_ss.at[d, e], y_rs.at[d, e], 2 * at_y(d) + core, aux,
        )

    def x_copy(e, f):
        return copy(
            x_out.at[piece_of(at_x(e), at_z(f))], x_in.at[e, pl.ds(pl.multiple_of(at_z(f) * piece, 8), piece)],
            x_ss.at[e, f], x_rs.at[e, f], occ, z * nx + at_x(e),
        )

    def z_copy(f):
        return copy(
            z_out.at[f], z_in.at[f], z_ss.at[f], z_rs.at[f], occ, at_z(f) * nx + x,
        )

    def gz_copy(f):
        mine = gram_ref.at[piece_of(x, z)]
        return copy(mine, mine, gz_ss.at[f], gz_rs.at[f], occ, at_z(f) * nx + x)

    def gz_in(f):
        theirs = gram_ref.at[piece_of(x, lax.rem(z + nz - f, nz))]
        return copy(theirs, theirs, gz_ss.at[f], gz_rs.at[f], occ, at_z(f) * nx + x)

    def gx_copy(e, f):
        part = gram_ref.at[piece_of(x, lax.rem(z + nz - f, nz))]
        return copy(part, part, gx_ss.at[e, f], gx_rs.at[e, f], occ, z * nx + at_x(e))

    def gx_in(e, f):
        part = gram_ref.at[piece_of(lax.rem(x + nx - e, nx), lax.rem(z + nz - f, nz))]
        return copy(part, part, gx_ss.at[e, f], gx_rs.at[e, f], occ, z * nx + at_x(e))

    half = domain // 2

    def row_copy(d, swap, h):
        target = 2 * at_y(d) + (other if swap else core)
        span = pl.ds(h * half, half)
        return copy(
            pad_buf.at[target, span], own_ref.at[occ, span],
            row_ss.at[d, swap, h], row_rs.at[d, swap, h], target, aux,
        )

    def row_in(d, swap, h):
        source = 2 * lax.rem(y + ny - d, ny) + (other if swap else core)
        span = pl.ds(h * half, half)
        return copy(
            pad_buf.at[source, span], own_ref.at[source, span],
            row_ss.at[d, swap, h], row_rs.at[d, swap, h], source, aux,
        )

    def gather(g):
        orbital = slot_ref[g]
        length = len_ref[orbital]
        for k in range(blocks):
            rows = pair_buf[orbital * blocks + k]
            pad_buf[g, k * size:(k + 1) * size, :] = jnp.where(k < length, rows, jnp.zeros_like(rows))

    def gram(g):
        place = 0
        for i in range(blocks):
            band = lax.dot_general(
                pad_buf[g, i * size:(i + 1) * size, :],
                pad_buf[g, :(i + 1) * size, :],
                (((1,), (1,)), ((), ())),
                preferred_element_type=F32,
            )
            for j in range(i + 1):
                part_ref[g, place * size:(place + 1) * size, :] = band[:, j * size:(j + 1) * size]
                place += 1

    early = [(d, 0, 0) for d in range(1, ny)]
    late = [(d, 0, 1) for d in range(1, ny)] + [(d, 1, h) for d in far_y for h in (0, 1)]
    for g in range(groups):
        load(g).wait()
    for d in range(1, ny):
        gather(2 * at_y(d) + core)
        row_copy(d, 0, 0).start()
    for d in far_y:
        gather(2 * at_y(d) + other)
        gram(2 * at_y(d) + other)
        for e in far_x:
            core_copy(d, e).start()
    for d in range(1, ny):
        gram(2 * at_y(d) + core)
    for e in far_x:
        for d in range(1, ny):
            core_copy(d, e).wait_recv()
            y_out[d, chunk_of(e), :] = part_ref[2 * at_y(d) + core, chunk_of(e), :] + core_buf[d, chunk_of(e), :]
            y_copy(d, e).start()
    for move in late:
        row_copy(*move).start()
    gather(occ)
    mine = pltpu.make_async_copy(pad_buf.at[occ], own_ref.at[occ], mine_sem)
    mine.start()
    gram(occ)
    for e in far_x:
        core_copy(0, e).wait_recv()
        for d in range(1, ny):
            y_copy(d, e).wait_recv()
        for f in far_z:
            if e:
                span = piece_of(at_x(e), at_z(f))
                total = part_ref[occ, span, :] + core_buf[0, span, :]
                for d in range(1, ny):
                    total = total + y_in[d, span, :]
                x_out[span, :] = total
                x_copy(e, f).start()
    for f in far_z:
        span = piece_of(x, at_z(f))
        total = part_ref[occ, span, :] + core_buf[0, span, :]
        for d in range(1, ny):
            total = total + y_in[d, span, :]
        for e in range(1, nx):
            x_copy(e, f).wait_recv()
            total = total + x_in[e, pl.ds(pl.multiple_of(at_z(f) * piece, 8), piece), :]
        if f:
            z_out[f] = total
            z_copy(f).start()
        else:
            z_out[0] = total
    total = z_out[0]
    for f in range(1, nz):
        z_copy(f).wait_recv()
        total = total + z_in[f]
    gram_ref[piece_of(x, z), :] = total
    for f in range(1, nz):
        gz_copy(f).start()
    for e in range(1, nx):
        gx_copy(e, 0).start()
    for f in range(1, nz):
        gz_in(f).wait_recv()
        for e in range(1, nx):
            gx_copy(e, f).start()
    for e in range(1, nx):
        for f in range(nz):
            gx_in(e, f).wait_recv()
    for move in early + late:
        row_in(*move).wait_recv()
    mine.wait()

    for d in far_y:
        for e in far_x:
            core_copy(d, e).wait_send()
            if d:
                y_copy(d, e).wait_send()
    for f in far_z:
        for e in range(1, nx):
            x_copy(e, f).wait_send()
            gx_copy(e, f).wait_send()
        if f:
            z_copy(f).wait_send()
            gz_copy(f).wait_send()
    for move in early + late:
        row_copy(*move).wait_send()


def exchange(slot_orbital, domain_len, pair_ints, blocks, n_aux):
    groups = slot_orbital.shape[0]
    _, lanes, cols = pair_ints.shape
    height = blocks * (blocks + 1) // 2 * lanes
    ny = groups // 2
    nx = ny if n_aux % ny == 0 else 1
    nz = n_aux // nx
    piece = height // n_aux
    dma = pltpu.SemaphoreType.DMA
    sems = [(ny, nx)] * 4 + [(nx, nz)] * 2 + [(nz,)] * 4 + [(nx, nz)] * 2 + [(ny, 2, 2)] * 2
    sems += [(groups,), ()]
    smem = pl.BlockSpec(memory_space=pltpu.SMEM)
    hbm = pl.BlockSpec(memory_space=pl.ANY)
    return pl.pallas_call(
        functools.partial(exchange_kernel, ny, nx, nz),
        out_shape=(
            jax.ShapeDtypeStruct((height, lanes), F32),
            jax.ShapeDtypeStruct((groups, blocks * lanes, cols), BF16),
        ),
        in_specs=[smem, smem, hbm],
        out_specs=[pl.BlockSpec(memory_space=pltpu.VMEM), hbm],
        scratch_shapes=[
            pltpu.VMEM(pair_ints.shape, BF16),
            pltpu.VMEM((groups, blocks * lanes, cols), BF16),
            pltpu.VMEM((groups, height, lanes), F32),
            pltpu.VMEM((ny, height, lanes), F32),
            pltpu.VMEM((ny, height, lanes), F32),
            pltpu.VMEM((ny, height, lanes), F32),
            pltpu.VMEM((height, lanes), F32),
            pltpu.VMEM((nx, piece * nz, lanes), F32),
            pltpu.VMEM((nz, piece, lanes), F32),
            pltpu.VMEM((nz, piece, lanes), F32),
        ] + [dma(shape) for shape in sems],
        compiler_params=pltpu.CompilerParams(
            collective_id=0, has_side_effects=True, vmem_limit_bytes=48 << 20
        ),
        name="exchange",
    )(slot_orbital, domain_len, pair_ints)


def solve_kernel(
    slot_ref, len_ref, block_ref, occ_ref, packed_ref, energy_hbm, own_hbm, out_hbm,
    m_high, m_low, x_ref, r_ref, rows_buf, out_buf, energy_buf, in_sem, out_sem, energy_sem,
):
    size = x_ref.shape[0]
    tiles, _, width = out_buf.shape
    blocks, _, side = energy_buf.shape
    me = lax.axis_index("occ")
    orbital = slot_ref[me]

    def energy(k):
        return pltpu.make_async_copy(
            energy_hbm.at[block_ref[orbital, k]], energy_buf.at[k], energy_sem.at[k]
        )

    def fetch(t):
        return pltpu.make_async_copy(own_hbm.at[t], rows_buf.at[t], in_sem.at[t])

    def flush(t):
        return pltpu.make_async_copy(
            out_buf.at[t], out_hbm.at[:, pl.ds(t * width, width)], out_sem.at[t]
        )

    for k in range(blocks):
        energy(k).start()
    for t in range(tiles):
        fetch(t).start()
    for k in range(blocks):
        energy(k).wait()
    place = 0
    for i in range(blocks):
        column = jnp.broadcast_to(energy_buf[i], (side, side)).T
        for j in range(i + 1):
            level = column + jnp.broadcast_to(energy_buf[j], (side, side)) - 2.0 * occ_ref[orbital]
            part = packed_ref[place * side:(place + 1) * side, :] / level
            x_ref[i * side:(i + 1) * side, j * side:(j + 1) * side] = part
            if j < i:
                x_ref[j * side:(j + 1) * side, i * side:(i + 1) * side] = part.T
            place += 1

    eye = (
        lax.broadcasted_iota(jnp.int32, (size, size), 0)
        == lax.broadcasted_iota(jnp.int32, (size, size), 1)
    ).astype(F32)
    amplitude = x_ref[...]
    trace = jnp.sum(amplitude * eye)
    live = (side * len_ref[orbital]).astype(F32)
    level_shift = LEVEL_RATIO * (trace / live + EPSILON)
    row_sum = jnp.max(jnp.sum(jnp.abs(amplitude), axis=0, keepdims=True))
    upper = level_shift + 1.01 * jnp.minimum(row_sum, 1.01 * trace)
    unit = 2.0 / (level_shift + upper)
    start = level_shift * unit
    scaled = (amplitude + level_shift * eye) * unit
    high, low = split(scaled)
    m_high[...] = high
    m_low[...] = low

    def factor(rho):
        return 2.0 / (1.0 + rho * (2.0 - rho))

    def advance(rho):
        return factor(rho) * rho * (2.0 - rho)

    x_ref[...] = factor(start) * (2.0 * eye - scaled)

    def quick(rho):
        x = x_ref[...]
        xb = x.astype(BF16)
        t = dot(m_high[...], xb)
        x_ref[...] = factor(rho) * (2.0 * x - dot(xb, t.astype(BF16)))
        return advance(rho)

    rho = lax.while_loop(lambda rho: rho < 0.95, quick, advance(start))
    del rho

    def times_m(x):
        xh, xl = split(x)
        mh = m_high[...]
        return dot(mh, xh) + (dot(mh, xl) + dot(m_low[...], xh))

    def residual():
        r = eye_again() - times_m(x_ref[...])
        r_ref[...] = r
        return jnp.sum(r * r)

    def eye_again():
        return (
            lax.broadcasted_iota(jnp.int32, (size, size), 0)
            == lax.broadcasted_iota(jnp.int32, (size, size), 1)
        ).astype(F32)

    def x_times(value):
        xh, xl = split(x_ref[...])
        vh, vl = split(value)
        return dot(xh, vh) + (dot(xh, vl) + dot(xl, vh))

    norm = residual()

    def careful(rho):
        x_ref[...] = factor(rho) * (2.0 * x_ref[...] - x_times(times_m(x_ref[...])))
        return advance(rho)

    def restart(_):
        x_ref[...] = eye_again()
        lax.while_loop(lambda rho: rho < 0.9999, careful, start)
        return residual()

    norm = lax.cond(norm < 0.9, lambda n: n, restart, norm)

    def refine(state):
        _, step = state
        x_ref[...] = x_ref[...] + x_times(r_ref[...])
        return residual(), step + 1

    lax.while_loop(
        lambda state: jnp.logical_and(state[0] > 1e-6, state[1] < 12), refine, (norm, 0)
    )
    x = x_ref[...] + x_times(r_ref[...])
    projector = (eye_again() - (level_shift * unit) * x).astype(BF16)
    m_high[...] = projector
    for t in range(tiles):
        fetch(t).wait()
        out_buf[t] = dot(m_high[...], rows_buf[t]).astype(BF16)
        flush(t).start()
    for t in range(tiles):
        flush(t).wait()


def solve_and_project(slot_orbital, domain_len, domain_blocks, occ_energy, packed, table, own):
    groups, size, width = own.shape
    blocks = domain_blocks.shape[1]
    side = size // blocks
    vmem = pl.BlockSpec(memory_space=pltpu.VMEM)
    smem = pl.BlockSpec(memory_space=pltpu.SMEM)
    hbm = pl.BlockSpec(memory_space=pl.ANY)
    return pl.pallas_call(
        solve_kernel,
        out_shape=jax.ShapeDtypeStruct((size, groups * width), BF16),
        in_specs=[smem] * 4 + [vmem] + [hbm] * 2,
        out_specs=hbm,
        scratch_shapes=[
            pltpu.VMEM((size, size), BF16),
            pltpu.VMEM((size, size), BF16),
            pltpu.VMEM((size, size), F32),
            pltpu.VMEM((size, size), F32),
            pltpu.VMEM((groups, size, width), BF16),
            pltpu.VMEM((groups, size, width), BF16),
            pltpu.VMEM((blocks, 1, side), F32),
            pltpu.SemaphoreType.DMA((groups,)),
            pltpu.SemaphoreType.DMA((groups,)),
            pltpu.SemaphoreType.DMA((blocks,)),
        ],
        compiler_params=pltpu.CompilerParams(vmem_limit_bytes=48 << 20),
        name="solve",
    )(slot_orbital, domain_len, domain_blocks, occ_energy, packed, table, own)


def solution(mesh):
    n_aux = mesh.shape["aux"]

    def local(pair_ints, domain_len, domain_blocks, slot_orbital, virt_energy, occ_energy):
        blocks = domain_blocks.shape[1]
        gram, own = exchange(slot_orbital, domain_len, pair_ints, blocks, n_aux)
        table = virt_energy.reshape(-1, 1, pair_ints.shape[1])
        return solve_and_project(
            slot_orbital, domain_len, domain_blocks, occ_energy, gram, table, own
        )[None]

    placed = (P(None, None, ("aux", "occ")), P(), P(), P(), P(), P())
    return jax.shard_map(
        local, mesh=mesh, in_specs=placed, out_specs=P("occ", None, "aux"), check_vma=False
    )
```

```python
import functools

import jax
import jax.numpy as jnp
from jax import lax
from jax.experimental import pallas as pl
from jax.experimental.pallas import tpu as pltpu
from jax.sharding import PartitionSpec as P

LEVEL_RATIO = 0.5
EPSILON = 1e-05
F32 = jnp.float32
BF16 = jnp.bfloat16


def split(value):
    high = value.astype(BF16)
    return high, (value - high.astype(F32)).astype(BF16)


def dot(a, b):
    return jnp.dot(a, b, preferred_element_type=F32)


def diagonal(size):
    return (
        lax.broadcasted_iota(jnp.int32, (size, size), 0)
        == lax.broadcasted_iota(jnp.int32, (size, size), 1)
    ).astype(F32)


def factor(rho):
    return 2.0 / (1.0 + rho * (2.0 - rho))


def advance(rho):
    return factor(rho) * rho * (2.0 - rho)


def prepare(energy, blocks, occ_level, live, packed_ref, m_high, m_low, x_ref):
    size = x_ref.shape[0]
    side = size // blocks
    place = 0
    for i in range(blocks):
        column = jnp.broadcast_to(energy(i), (side, side)).T
        for j in range(i + 1):
            level = column + jnp.broadcast_to(energy(j), (side, side)) - 2.0 * occ_level
            part = packed_ref[place * side:(place + 1) * side, :] / level
            x_ref[i * side:(i + 1) * side, j * side:(j + 1) * side] = part
            if j < i:
                x_ref[j * side:(j + 1) * side, i * side:(i + 1) * side] = part.T
            place += 1
    eye = diagonal(size)
    amplitude = x_ref[...]
    trace = jnp.sum(amplitude * eye)
    level_shift = LEVEL_RATIO * (trace / live + EPSILON)
    row_sum = jnp.max(jnp.sum(jnp.abs(amplitude), axis=0, keepdims=True))
    upper = level_shift + 1.01 * jnp.minimum(row_sum, 1.01 * trace)
    unit = 2.0 / (level_shift + upper)
    start = level_shift * unit
    scaled = (amplitude + level_shift * eye) * unit
    high, low = split(scaled)
    m_high[...] = high
    m_low[...] = low
    x_ref[...] = factor(start) * (2.0 * eye - scaled)
    return start


def times_m(m_high, m_low, x):
    xh, xl = split(x)
    mh = m_high[...]
    return dot(mh, xh) + (dot(mh, xl) + dot(m_low[...], xh))


def x_times(x, value):
    xh, xl = split(x)
    vh, vl = split(value)
    return dot(xh, vh) + (dot(xh, vl) + dot(xl, vh))


def residual(m_high, m_low, x_ref, r_ref):
    r = diagonal(x_ref.shape[0]) - times_m(m_high, m_low, x_ref[...])
    r_ref[...] = r
    return jnp.sum(r * r)


def quick(m_high, x_ref, rho):
    x = x_ref[...]
    xb = x.astype(BF16)
    t = dot(m_high[...], xb)
    x_ref[...] = factor(rho) * (2.0 * x - dot(xb, t.astype(BF16)))
    return advance(rho)


QUICK_STEPS = 5
RESIDUAL_BOUND = 1e-6


def invert_fixed(start, m_high, m_low, x_ref, r_ref):
    lax.fori_loop(0, QUICK_STEPS, lambda _, rho: quick(m_high, x_ref, rho), advance(start))
    residual(m_high, m_low, x_ref, r_ref)
    x = x_ref[...]
    x_ref[...] = x + dot(x.astype(BF16), r_ref[...].astype(BF16))
    residual(m_high, m_low, x_ref, r_ref)
    x = x_ref[...]
    x_ref[...] = x + x_times(x, r_ref[...])
    norm = residual(m_high, m_low, x_ref, r_ref)
    x = x_ref[...]
    x = x + dot(x.astype(BF16), r_ref[...].astype(BF16))
    return diagonal(x.shape[0]) - start * x, norm


def invert_checked(start, m_high, m_low, x_ref, r_ref):
    def careful(rho):
        x = x_ref[...]
        x_ref[...] = factor(rho) * (2.0 * x - x_times(x, times_m(m_high, m_low, x)))
        return advance(rho)

    lax.while_loop(lambda rho: rho < 0.9999, careful, advance(start))

    def refine(state):
        x_ref[...] = x_ref[...] + x_times(x_ref[...], r_ref[...])
        return residual(m_high, m_low, x_ref, r_ref), state[1] + 1

    lax.while_loop(
        lambda state: jnp.logical_and(state[0] > RESIDUAL_BOUND, state[1] < 12),
        refine,
        (residual(m_high, m_low, x_ref, r_ref), 0),
    )
    x = x_ref[...] + x_times(x_ref[...], r_ref[...])
    return diagonal(x.shape[0]) - start * x


MESH = pl.DeviceIdType.MESH


def exchange_kernel(
    ny, nx, nz, slot_ref, len_ref, block_ref, occ_ref, energy_ref, pair_hbm,
    gram_ref, own_ref, filter_ref, norm_ref, m_high, m_low, x_ref, r_ref, pair_buf, pad_buf, part_ref, core_buf, y_out, y_in, x_out, x_in, z_out, z_in,
    core_ss, core_rs, y_ss, y_rs, x_ss, x_rs, z_ss, z_rs,
    gz_ss, gz_rs, gx_ss, gx_rs, row_ss, row_rs, pair_sem, mine_sem,
):
    occ, aux = lax.axis_index("occ"), lax.axis_index("aux")
    y, core = lax.div(occ, 2), lax.rem(occ, 2)
    z, x = lax.div(aux, nx), lax.rem(aux, nx)
    piece = gram_ref.shape[0] // (nx * nz)
    chunk = piece * nz
    other = 1 - core

    def at_y(d):
        return lax.rem(y + d, ny)

    def at_x(e):
        return lax.rem(x + e, nx)

    def at_z(f):
        return lax.rem(z + f, nz)

    def chunk_of(e):
        return pl.ds(pl.multiple_of(at_x(e) * chunk, 8), chunk)

    def piece_of(xx, zz):
        return pl.ds(pl.multiple_of((xx * nz + zz) * piece, 8), piece)

    def copy(src, dst, ss, rs, to_occ, to_aux):
        return pltpu.make_async_remote_copy(
            src_ref=src, dst_ref=dst, send_sem=ss, recv_sem=rs,
            device_id=(to_occ, to_aux), device_id_type=MESH,
        )

    groups, domain, _ = pad_buf.shape
    size = pair_buf.shape[1]
    blocks = domain // size

    def load(g):
        span = pl.ds(g * blocks, blocks)
        return pltpu.make_async_copy(pair_hbm.at[span], pair_buf.at[span], pair_sem.at[g])

    for g in range(groups):
        load(g).start()
    barrier = pltpu.get_barrier_semaphore()
    peers = [(2 * y + other, aux)]
    for d in range(1, ny):
        peers += [(2 * at_y(d) + core, aux), (2 * at_y(d) + other, aux)]
    peers += [(occ, z * nx + at_x(e)) for e in range(1, nx)]
    peers += [(occ, at_z(f) * nx + x) for f in range(1, nz)]
    for peer in peers:
        pl.semaphore_signal(barrier, inc=1, device_id=peer, device_id_type=MESH)
    pl.semaphore_wait(barrier, len(peers))

    far_y = list(range(1, ny)) + [0]
    far_x = list(range(1, nx)) + [0]
    far_z = list(range(1, nz)) + [0]

    def core_copy(d, e):
        return copy(
            part_ref.at[2 * at_y(d) + other, chunk_of(e)], core_buf.at[d, chunk_of(e)],
            core_ss.at[d, e], core_rs.at[d, e], 2 * y + other, aux,
        )

    def y_copy(d, e):
        return copy(
            y_out.at[d, chunk_of(e)], y_in.at[d, chunk_of(e)],
            y_ss.at[d, e], y_rs.at[d, e], 2 * at_y(d) + core, aux,
        )

    def x_copy(e, f):
        return copy(
            x_out.at[piece_of(at_x(e), at_z(f))], x_in.at[e, pl.ds(pl.multiple_of(at_z(f) * piece, 8), piece)],
            x_ss.at[e, f], x_rs.at[e, f], occ, z * nx + at_x(e),
        )

    def z_copy(f):
        return copy(
            z_out.at[f], z_in.at[f], z_ss.at[f], z_rs.at[f], occ, at_z(f) * nx + x,
        )

    def gz_copy(f):
        mine = gram_ref.at[piece_of(x, z)]
        return copy(mine, mine, gz_ss.at[f], gz_rs.at[f], occ, at_z(f) * nx + x)

    def gz_in(f):
        theirs = gram_ref.at[piece_of(x, lax.rem(z + nz - f, nz))]
        return copy(theirs, theirs, gz_ss.at[f], gz_rs.at[f], occ, at_z(f) * nx + x)

    def gx_copy(e, f):
        part = gram_ref.at[piece_of(x, lax.rem(z + nz - f, nz))]
        return copy(part, part, gx_ss.at[e, f], gx_rs.at[e, f], occ, z * nx + at_x(e))

    def gx_in(e, f):
        part = gram_ref.at[piece_of(lax.rem(x + nx - e, nx), lax.rem(z + nz - f, nz))]
        return copy(part, part, gx_ss.at[e, f], gx_rs.at[e, f], occ, z * nx + at_x(e))

    half = domain // 2

    def row_copy(d, swap, h):
        target = 2 * at_y(d) + (other if swap else core)
        span = pl.ds(h * half, half)
        return copy(
            pad_buf.at[target, span], own_ref.at[occ, span],
            row_ss.at[d, swap, h], row_rs.at[d, swap, h], target, aux,
        )

    def row_in(d, swap, h):
        source = 2 * lax.rem(y + ny - d, ny) + (other if swap else core)
        span = pl.ds(h * half, half)
        return copy(
            pad_buf.at[source, span], own_ref.at[source, span],
            row_ss.at[d, swap, h], row_rs.at[d, swap, h], source, aux,
        )

    def gather(g):
        orbital = slot_ref[g]
        length = len_ref[orbital]
        for k in range(blocks):
            rows = pair_buf[orbital * blocks + k]
            pad_buf[g, k * size:(k + 1) * size, :] = jnp.where(k < length, rows, jnp.zeros_like(rows))

    def gram(g):
        place = 0
        for i in range(blocks):
            band = lax.dot_general(
                pad_buf[g, i * size:(i + 1) * size, :],
                pad_buf[g, :(i + 1) * size, :],
                (((1,), (1,)), ((), ())),
                preferred_element_type=F32,
            )
            for j in range(i + 1):
                part_ref[g, place * size:(place + 1) * size, :] = band[:, j * size:(j + 1) * size]
                place += 1

    early = [(d, 0, 0) for d in range(1, ny)]
    late = [(d, 0, 1) for d in range(1, ny)] + [(d, 1, h) for d in far_y for h in (0, 1)]
    for g in range(groups):
        load(g).wait()
    for d in range(1, ny):
        gather(2 * at_y(d) + core)
        row_copy(d, 0, 0).start()
    for d in far_y:
        gather(2 * at_y(d) + other)
        gram(2 * at_y(d) + other)
        for e in far_x:
            core_copy(d, e).start()
    for d in range(1, ny):
        gram(2 * at_y(d) + core)
    for e in far_x:
        for d in range(1, ny):
            core_copy(d, e).wait_recv()
            y_out[d, chunk_of(e), :] = part_ref[2 * at_y(d) + core, chunk_of(e), :] + core_buf[d, chunk_of(e), :]
            y_copy(d, e).start()
    for move in late:
        row_copy(*move).start()
    gather(occ)
    mine = pltpu.make_async_copy(pad_buf.at[occ], own_ref.at[occ], mine_sem)
    mine.start()
    gram(occ)
    for e in far_x:
        core_copy(0, e).wait_recv()
        for d in range(1, ny):
            y_copy(d, e).wait_recv()
        for f in far_z:
            if e:
                span = piece_of(at_x(e), at_z(f))
                total = part_ref[occ, span, :] + core_buf[0, span, :]
                for d in range(1, ny):
                    total = total + y_in[d, span, :]
                x_out[span, :] = total
                x_copy(e, f).start()
    for f in far_z:
        span = piece_of(x, at_z(f))
        total = part_ref[occ, span, :] + core_buf[0, span, :]
        for d in range(1, ny):
            total = total + y_in[d, span, :]
        for e in range(1, nx):
            x_copy(e, f).wait_recv()
            total = total + x_in[e, pl.ds(pl.multiple_of(at_z(f) * piece, 8), piece), :]
        if f:
            z_out[f] = total
            z_copy(f).start()
        else:
            z_out[0] = total
    total = z_out[0]
    for f in range(1, nz):
        z_copy(f).wait_recv()
        total = total + z_in[f]
    gram_ref[piece_of(x, z), :] = total
    for f in range(1, nz):
        gz_copy(f).start()
    for e in range(1, nx):
        gx_copy(e, 0).start()
    for f in range(1, nz):
        gz_in(f).wait_recv()
        for e in range(1, nx):
            gx_copy(e, f).start()
    for e in range(1, nx):
        for f in range(nz):
            gx_in(e, f).wait_recv()
    orbital = slot_ref[occ]
    start = prepare(
        lambda k: energy_ref[block_ref[orbital, k]], blocks, occ_ref[orbital],
        (size * len_ref[orbital]).astype(F32), gram_ref, m_high, m_low, x_ref,
    )
    projector, norm = invert_fixed(start, m_high, m_low, x_ref, r_ref)
    filter_ref[...] = projector.astype(BF16)
    norm_ref[...] = jnp.full(norm_ref.shape, norm, F32)
    for move in early + late:
        row_in(*move).wait_recv()
    mine.wait()

    for d in far_y:
        for e in far_x:
            core_copy(d, e).wait_send()
            if d:
                y_copy(d, e).wait_send()
    for f in far_z:
        for e in range(1, nx):
            x_copy(e, f).wait_send()
            gx_copy(e, f).wait_send()
        if f:
            z_copy(f).wait_send()
            gz_copy(f).wait_send()
    for move in early + late:
        row_copy(*move).wait_send()


def exchange(slot_orbital, domain_len, domain_blocks, occ_energy, table, pair_ints, n_aux):
    blocks = domain_blocks.shape[1]
    domain = blocks * pair_ints.shape[1]
    groups = slot_orbital.shape[0]
    _, lanes, cols = pair_ints.shape
    height = blocks * (blocks + 1) // 2 * lanes
    ny = groups // 2
    nx = ny if n_aux % ny == 0 else 1
    nz = n_aux // nx
    piece = height // n_aux
    dma = pltpu.SemaphoreType.DMA
    sems = [(ny, nx)] * 4 + [(nx, nz)] * 2 + [(nz,)] * 4 + [(nx, nz)] * 2 + [(ny, 2, 2)] * 2
    sems += [(groups,), ()]
    smem = pl.BlockSpec(memory_space=pltpu.SMEM)
    vmem = pl.BlockSpec(memory_space=pltpu.VMEM)
    return pl.pallas_call(
        functools.partial(exchange_kernel, ny, nx, nz),
        out_shape=(
            jax.ShapeDtypeStruct((height, lanes), F32),
            jax.ShapeDtypeStruct((groups, domain, cols), BF16),
            jax.ShapeDtypeStruct((domain, domain), BF16),
            jax.ShapeDtypeStruct((8, lanes), F32),
        ),
        in_specs=[smem] * 4 + [vmem, pl.BlockSpec(memory_space=pltpu.HBM)],
        out_specs=[vmem] * 4,
        scratch_shapes=[
            pltpu.VMEM((domain, domain), BF16),
            pltpu.VMEM((domain, domain), BF16),
            pltpu.VMEM((domain, domain), F32),
            pltpu.VMEM((domain, domain), F32),
            pltpu.VMEM(pair_ints.shape, BF16),
            pltpu.VMEM((groups, blocks * lanes, cols), BF16),
            pltpu.VMEM((groups, height, lanes), F32),
            pltpu.VMEM((ny, height, lanes), F32),
            pltpu.VMEM((ny, height, lanes), F32),
            pltpu.VMEM((ny, height, lanes), F32),
            pltpu.VMEM((height, lanes), F32),
            pltpu.VMEM((nx, piece * nz, lanes), F32),
            pltpu.VMEM((nz, piece, lanes), F32),
            pltpu.VMEM((nz, piece, lanes), F32),
        ] + [dma(shape) for shape in sems],
        compiler_params=pltpu.CompilerParams(
            collective_id=0, has_side_effects=True, vmem_limit_bytes=48 << 20
        ),
        name="exchange",
    )(slot_orbital, domain_len, domain_blocks, occ_energy, table, pair_ints)


def project_kernel(
    slot_ref, len_ref, block_ref, occ_ref, packed_ref, own_ref, filter_ref, norm_ref, energy_hbm, out_hbm,
    m_high, m_low, x_ref, r_ref, out_buf, energy_buf, out_sem, energy_sem,
):
    tiles, _, width = out_buf.shape
    blocks, _, side = energy_buf.shape
    orbital = slot_ref[lax.axis_index("occ")]
    good = jnp.max(norm_ref[...]) < RESIDUAL_BOUND

    @pl.when(good)
    def _():
        m_high[...] = filter_ref[...]

    @pl.when(jnp.logical_not(good))
    def _():
        def energy(k):
            return pltpu.make_async_copy(
                energy_hbm.at[block_ref[orbital, k]], energy_buf.at[k], energy_sem.at[k]
            )

        for k in range(blocks):
            energy(k).start()
        for k in range(blocks):
            energy(k).wait()
        live = (side * len_ref[orbital]).astype(F32)
        start = prepare(
            lambda k: energy_buf[k], blocks, occ_ref[orbital], live, packed_ref, m_high, m_low, x_ref
        )
        m_high[...] = invert_checked(start, m_high, m_low, x_ref, r_ref).astype(BF16)

    def flush(t):
        return pltpu.make_async_copy(
            out_buf.at[t], out_hbm.at[:, pl.ds(t * width, width)], out_sem.at[t]
        )

    for t in range(tiles):
        out_buf[t] = dot(m_high[...], own_ref[t]).astype(BF16)
        flush(t).start()
    for t in range(tiles):
        flush(t).wait()


def project(slot_orbital, domain_len, domain_blocks, occ_energy, packed, own, projector, norm, table):
    groups, size, width = own.shape
    blocks = domain_blocks.shape[1]
    side = size // blocks
    vmem = pl.BlockSpec(memory_space=pltpu.VMEM)
    smem = pl.BlockSpec(memory_space=pltpu.SMEM)
    return pl.pallas_call(
        project_kernel,
        out_shape=jax.ShapeDtypeStruct((size, groups * width), BF16),
        in_specs=[smem] * 4 + [vmem] * 4 + [pl.BlockSpec(memory_space=pl.ANY)],
        out_specs=pl.BlockSpec(memory_space=pl.ANY),
        scratch_shapes=[
            pltpu.VMEM((size, size), BF16),
            pltpu.VMEM((size, size), BF16),
            pltpu.VMEM((size, size), F32),
            pltpu.VMEM((size, size), F32),
            pltpu.VMEM((groups, size, width), BF16),
            pltpu.VMEM((blocks, 1, side), F32),
            pltpu.SemaphoreType.DMA((groups,)),
            pltpu.SemaphoreType.DMA((blocks,)),
        ],
        compiler_params=pltpu.CompilerParams(vmem_limit_bytes=24 << 20),
        name="project",
    )(slot_orbital, domain_len, domain_blocks, occ_energy, packed, own, projector, norm, table)


def solution(mesh):
    n_aux = mesh.shape["aux"]

    def local(pair_ints, domain_len, domain_blocks, slot_orbital, virt_energy, occ_energy):
        table = virt_energy.reshape(-1, 1, pair_ints.shape[1])
        gram, own, projector, norm = exchange(
            slot_orbital, domain_len, domain_blocks, occ_energy, table, pair_ints, n_aux
        )
        return project(
            slot_orbital, domain_len, domain_blocks, occ_energy, gram, own, projector, norm, table
        )[None]

    placed = (P(None, None, ("aux", "occ")), P(), P(), P(), P(), P())
    return jax.shard_map(
        local, mesh=mesh, in_specs=placed, out_specs=P("occ", None, "aux"), check_vma=False
    )
```

```python
import functools

import jax
import jax.numpy as jnp
from jax import lax
from jax.experimental import pallas as pl
from jax.experimental.pallas import tpu as pltpu
from jax.sharding import PartitionSpec as P

LEVEL_RATIO = 0.5
EPSILON = 1e-05
F32 = jnp.float32
BF16 = jnp.bfloat16


def split(value):
    high = value.astype(BF16)
    return high, (value - high.astype(F32)).astype(BF16)


def dot(a, b):
    return jnp.dot(a, b, preferred_element_type=F32)


def diagonal(size):
    return (
        lax.broadcasted_iota(jnp.int32, (size, size), 0)
        == lax.broadcasted_iota(jnp.int32, (size, size), 1)
    ).astype(F32)


def factor(rho):
    return 2.0 / (1.0 + rho * (2.0 - rho))


def advance(rho):
    return factor(rho) * rho * (2.0 - rho)


def prepare(energy, blocks, occ_level, live, packed_ref, m_high, m_low, x_ref):
    size = x_ref.shape[0]
    side = size // blocks
    place = 0
    for i in range(blocks):
        column = jnp.broadcast_to(energy(i), (side, side)).T
        for j in range(i + 1):
            level = column + jnp.broadcast_to(energy(j), (side, side)) - 2.0 * occ_level
            part = packed_ref[place * side:(place + 1) * side, :] / level
            x_ref[i * side:(i + 1) * side, j * side:(j + 1) * side] = part
            if j < i:
                x_ref[j * side:(j + 1) * side, i * side:(i + 1) * side] = part.T
            place += 1
    eye = diagonal(size)
    amplitude = x_ref[...]
    trace = jnp.sum(amplitude * eye)
    level_shift = LEVEL_RATIO * (trace / live + EPSILON)
    row_sum = jnp.max(jnp.sum(jnp.abs(amplitude), axis=0, keepdims=True))
    upper = level_shift + 1.01 * jnp.minimum(row_sum, 1.01 * trace)
    unit = 2.0 / (level_shift + upper)
    start = level_shift * unit
    scaled = (amplitude + level_shift * eye) * unit
    high, low = split(scaled)
    m_high[...] = high
    m_low[...] = low
    x_ref[...] = factor(start) * (2.0 * eye - scaled)
    return start


def times_m(m_high, m_low, x):
    xh, xl = split(x)
    mh = m_high[...]
    return dot(mh, xh) + (dot(mh, xl) + dot(m_low[...], xh))


def x_times(x, value):
    xh, xl = split(x)
    vh, vl = split(value)
    return dot(xh, vh) + (dot(xh, vl) + dot(xl, vh))


def residual(m_high, m_low, x_ref, r_ref):
    r = diagonal(x_ref.shape[0]) - times_m(m_high, m_low, x_ref[...])
    r_ref[...] = r
    return jnp.sum(r * r)


def quick(m_high, x_ref, rho):
    x = x_ref[...]
    xb = x.astype(BF16)
    t = dot(m_high[...], xb)
    x_ref[...] = factor(rho) * (2.0 * x - dot(xb, t.astype(BF16)))
    return advance(rho)


QUICK_STEPS = 5
PIECES = 4
RESIDUAL_BOUND = 1e-6


def invert_fixed(start, m_high, m_low, x_ref, r_ref):
    lax.fori_loop(0, QUICK_STEPS, lambda _, rho: quick(m_high, x_ref, rho), advance(start))
    residual(m_high, m_low, x_ref, r_ref)
    x = x_ref[...]
    x_ref[...] = x + dot(x.astype(BF16), r_ref[...].astype(BF16))
    residual(m_high, m_low, x_ref, r_ref)
    x = x_ref[...]
    x_ref[...] = x + x_times(x, r_ref[...])
    norm = residual(m_high, m_low, x_ref, r_ref)
    x = x_ref[...]
    x = x + dot(x.astype(BF16), r_ref[...].astype(BF16))
    return diagonal(x.shape[0]) - start * x, norm


def invert_checked(start, m_high, m_low, x_ref, r_ref):
    def careful(rho):
        x = x_ref[...]
        x_ref[...] = factor(rho) * (2.0 * x - x_times(x, times_m(m_high, m_low, x)))
        return advance(rho)

    lax.while_loop(lambda rho: rho < 0.9999, careful, advance(start))

    def refine(state):
        x_ref[...] = x_ref[...] + x_times(x_ref[...], r_ref[...])
        return residual(m_high, m_low, x_ref, r_ref), state[1] + 1

    lax.while_loop(
        lambda state: jnp.logical_and(state[0] > RESIDUAL_BOUND, state[1] < 12),
        refine,
        (residual(m_high, m_low, x_ref, r_ref), 0),
    )
    x = x_ref[...] + x_times(x_ref[...], r_ref[...])
    return diagonal(x.shape[0]) - start * x


MESH = pl.DeviceIdType.MESH


def exchange_kernel(
    ny, nx, nz, slot_hbm, len_hbm, block_hbm, occ_hbm, energy_hbm, pair_hbm,
    gram_ref, own_ref, filter_ref, norm_ref, slot_ref, len_ref, block_ref, occ_ref, energy_ref, small_sem,
    m_high, m_low, x_ref, r_ref, pair_buf, pad_buf, part_ref, core_buf, y_out, y_in, x_out, x_in, z_out, z_in,
    core_ss, core_rs, y_ss, y_rs, x_ss, x_rs, z_ss, z_rs,
    gz_ss, gz_rs, gx_ss, gx_rs, row_ss, row_rs, pair_sem, mine_sem,
):
    occ, aux = lax.axis_index("occ"), lax.axis_index("aux")
    y, core = lax.div(occ, 2), lax.rem(occ, 2)
    z, x = lax.div(aux, nx), lax.rem(aux, nx)
    piece = gram_ref.shape[0] // (nx * nz)
    chunk = piece * nz
    other = 1 - core

    def at_y(d):
        return lax.rem(y + d, ny)

    def at_x(e):
        return lax.rem(x + e, nx)

    def at_z(f):
        return lax.rem(z + f, nz)

    def chunk_of(e):
        return pl.ds(pl.multiple_of(at_x(e) * chunk, 8), chunk)

    def piece_of(xx, zz):
        return pl.ds(pl.multiple_of((xx * nz + zz) * piece, 8), piece)

    def copy(src, dst, ss, rs, to_occ, to_aux):
        return pltpu.make_async_remote_copy(
            src_ref=src, dst_ref=dst, send_sem=ss, recv_sem=rs,
            device_id=(to_occ, to_aux), device_id_type=MESH,
        )

    groups, domain, _ = pad_buf.shape
    size = pair_buf.shape[1]
    blocks = domain // size

    def load(g):
        span = pl.ds(g * blocks, blocks)
        return pltpu.make_async_copy(pair_hbm.at[span], pair_buf.at[span], pair_sem.at[g])

    small = [
        pltpu.make_async_copy(src, dst, small_sem.at[k])
        for k, (src, dst) in enumerate(
            [(slot_hbm, slot_ref), (len_hbm, len_ref), (block_hbm, block_ref), (occ_hbm, occ_ref),
             (energy_hbm, energy_ref)]
        )
    ]
    for k in (0, 1):
        small[k].start()
    for g in range(groups):
        load(g).start()
    for k in (2, 3, 4):
        small[k].start()
    barrier = pltpu.get_barrier_semaphore()
    peers = [(2 * y + other, aux)]
    for d in range(1, ny):
        peers += [(2 * at_y(d) + core, aux), (2 * at_y(d) + other, aux)]
    peers += [(occ, z * nx + at_x(e)) for e in range(1, nx)]
    peers += [(occ, at_z(f) * nx + x) for f in range(1, nz)]
    for peer in peers:
        pl.semaphore_signal(barrier, inc=1, device_id=peer, device_id_type=MESH)
    pl.semaphore_wait(barrier, len(peers))

    far_y = list(range(1, ny)) + [0]
    far_x = list(range(1, nx)) + [0]
    far_z = list(range(1, nz)) + [0]

    def core_copy(d, e):
        return copy(
            part_ref.at[2 * at_y(d) + other, chunk_of(e)], core_buf.at[d, chunk_of(e)],
            core_ss.at[d, e], core_rs.at[d, e], 2 * y + other, aux,
        )

    def y_copy(d, e):
        return copy(
            y_out.at[d, chunk_of(e)], y_in.at[d, chunk_of(e)],
            y_ss.at[d, e], y_rs.at[d, e], 2 * at_y(d) + core, aux,
        )

    def x_copy(e, f):
        return copy(
            x_out.at[piece_of(at_x(e), at_z(f))], x_in.at[e, pl.ds(pl.multiple_of(at_z(f) * piece, 8), piece)],
            x_ss.at[e, f], x_rs.at[e, f], occ, z * nx + at_x(e),
        )

    def z_copy(f):
        return copy(
            z_out.at[f], z_in.at[f], z_ss.at[f], z_rs.at[f], occ, at_z(f) * nx + x,
        )

    def gz_copy(f):
        mine = gram_ref.at[piece_of(x, z)]
        return copy(mine, mine, gz_ss.at[f], gz_rs.at[f], occ, at_z(f) * nx + x)

    def gz_in(f):
        theirs = gram_ref.at[piece_of(x, lax.rem(z + nz - f, nz))]
        return copy(theirs, theirs, gz_ss.at[f], gz_rs.at[f], occ, at_z(f) * nx + x)

    def gx_copy(e, f):
        part = gram_ref.at[piece_of(x, lax.rem(z + nz - f, nz))]
        return copy(part, part, gx_ss.at[e, f], gx_rs.at[e, f], occ, z * nx + at_x(e))

    def gx_in(e, f):
        part = gram_ref.at[piece_of(lax.rem(x + nx - e, nx), lax.rem(z + nz - f, nz))]
        return copy(part, part, gx_ss.at[e, f], gx_rs.at[e, f], occ, z * nx + at_x(e))

    half = domain // PIECES

    def row_copy(d, swap, h):
        target = 2 * at_y(d) + (other if swap else core)
        span = pl.ds(h * half, half)
        return copy(
            pad_buf.at[target, span], own_ref.at[occ, span],
            row_ss.at[d, swap, h], row_rs.at[d, swap, h], target, aux,
        )

    def row_in(d, swap, h):
        source = 2 * lax.rem(y + ny - d, ny) + (other if swap else core)
        span = pl.ds(h * half, half)
        return copy(
            pad_buf.at[source, span], own_ref.at[source, span],
            row_ss.at[d, swap, h], row_rs.at[d, swap, h], source, aux,
        )

    def gather(g):
        orbital = slot_ref[g]
        length = len_ref[orbital]
        for k in range(blocks):
            rows = pair_buf[orbital * blocks + k]
            pad_buf[g, k * size:(k + 1) * size, :] = jnp.where(k < length, rows, jnp.zeros_like(rows))

    def gram(g):
        place = 0
        for i in range(blocks):
            band = lax.dot_general(
                pad_buf[g, i * size:(i + 1) * size, :],
                pad_buf[g, :(i + 1) * size, :],
                (((1,), (1,)), ((), ())),
                preferred_element_type=F32,
            )
            for j in range(i + 1):
                part_ref[g, place * size:(place + 1) * size, :] = band[:, j * size:(j + 1) * size]
                place += 1

    early = [(d, 0, 0) for d in range(1, ny)]
    late = [(d, 0, h) for d in range(1, ny) for h in range(1, PIECES)]
    late += [(d, 1, h) for d in far_y for h in range(PIECES)]
    for k in range(5):
        small[k].wait()
    for g in range(groups):
        load(g).wait()
    for d in range(1, ny):
        gather(2 * at_y(d) + core)
        row_copy(d, 0, 0).start()
    for d in far_y:
        gather(2 * at_y(d) + other)
        gram(2 * at_y(d) + other)
        for e in far_x:
            core_copy(d, e).start()
    for d in range(1, ny):
        gram(2 * at_y(d) + core)
    for e in far_x:
        for d in range(1, ny):
            core_copy(d, e).wait_recv()
            y_out[d, chunk_of(e), :] = part_ref[2 * at_y(d) + core, chunk_of(e), :] + core_buf[d, chunk_of(e), :]
            y_copy(d, e).start()
    for move in late:
        row_copy(*move).start()
    gather(occ)
    mine = pltpu.make_async_copy(pad_buf.at[occ], own_ref.at[occ], mine_sem)
    mine.start()
    gram(occ)
    for e in far_x:
        core_copy(0, e).wait_recv()
        for d in range(1, ny):
            y_copy(d, e).wait_recv()
        for f in far_z:
            if e:
                span = piece_of(at_x(e), at_z(f))
                total = part_ref[occ, span, :] + core_buf[0, span, :]
                for d in range(1, ny):
                    total = total + y_in[d, span, :]
                x_out[span, :] = total
                x_copy(e, f).start()
    for f in far_z:
        span = piece_of(x, at_z(f))
        total = part_ref[occ, span, :] + core_buf[0, span, :]
        for d in range(1, ny):
            total = total + y_in[d, span, :]
        for e in range(1, nx):
            x_copy(e, f).wait_recv()
            total = total + x_in[e, pl.ds(pl.multiple_of(at_z(f) * piece, 8), piece), :]
        if f:
            z_out[f] = total
            z_copy(f).start()
        else:
            z_out[0] = total
    total = z_out[0]
    for f in range(1, nz):
        z_copy(f).wait_recv()
        total = total + z_in[f]
    gram_ref[piece_of(x, z), :] = total
    for f in range(1, nz):
        gz_copy(f).start()
    for e in range(1, nx):
        gx_copy(e, 0).start()
    for f in range(1, nz):
        gz_in(f).wait_recv()
        for e in range(1, nx):
            gx_copy(e, f).start()
    for e in range(1, nx):
        for f in range(nz):
            gx_in(e, f).wait_recv()
    orbital = slot_ref[occ]
    start = prepare(
        lambda k: energy_ref[block_ref[orbital, k]], blocks, occ_ref[orbital],
        (size * len_ref[orbital]).astype(F32), gram_ref, m_high, m_low, x_ref,
    )
    projector, norm = invert_fixed(start, m_high, m_low, x_ref, r_ref)
    filter_ref[...] = projector.astype(BF16)
    norm_ref[...] = jnp.full(norm_ref.shape, norm, F32)
    for move in early + late:
        row_in(*move).wait_recv()
    mine.wait()

    for d in far_y:
        for e in far_x:
            core_copy(d, e).wait_send()
            if d:
                y_copy(d, e).wait_send()
    for f in far_z:
        for e in range(1, nx):
            x_copy(e, f).wait_send()
            gx_copy(e, f).wait_send()
        if f:
            z_copy(f).wait_send()
            gz_copy(f).wait_send()
    for move in early + late:
        row_copy(*move).wait_send()


def exchange(slot_orbital, domain_len, domain_blocks, occ_energy, table, pair_ints, n_aux):
    blocks = domain_blocks.shape[1]
    domain = blocks * pair_ints.shape[1]
    groups = slot_orbital.shape[0]
    _, lanes, cols = pair_ints.shape
    height = blocks * (blocks + 1) // 2 * lanes
    ny = groups // 2
    nx = ny if n_aux % ny == 0 else 1
    nz = n_aux // nx
    piece = height // n_aux
    dma = pltpu.SemaphoreType.DMA
    sems = [(ny, nx)] * 4 + [(nx, nz)] * 2 + [(nz,)] * 4 + [(nx, nz)] * 2 + [(ny, 2, PIECES)] * 2
    sems += [(groups,), ()]
    hbm = pl.BlockSpec(memory_space=pltpu.HBM)
    vmem = pl.BlockSpec(memory_space=pltpu.VMEM)
    return pl.pallas_call(
        functools.partial(exchange_kernel, ny, nx, nz),
        out_shape=(
            jax.ShapeDtypeStruct((height, lanes), F32),
            jax.ShapeDtypeStruct((groups, domain, cols), BF16),
            jax.ShapeDtypeStruct((domain, domain), BF16),
            jax.ShapeDtypeStruct((8, lanes), F32),
        ),
        in_specs=[hbm] * 6,
        out_specs=[vmem, hbm, vmem, vmem],
        scratch_shapes=[
            pltpu.SMEM(slot_orbital.shape, jnp.int32),
            pltpu.SMEM(domain_len.shape, jnp.int32),
            pltpu.SMEM(domain_blocks.shape, jnp.int32),
            pltpu.SMEM(occ_energy.shape, F32),
            pltpu.VMEM(table.shape, F32),
            dma((5,)),
            pltpu.VMEM((domain, domain), BF16),
            pltpu.VMEM((domain, domain), BF16),
            pltpu.VMEM((domain, domain), F32),
            pltpu.VMEM((domain, domain), F32),
            pltpu.VMEM(pair_ints.shape, BF16),
            pltpu.VMEM((groups, blocks * lanes, cols), BF16),
            pltpu.VMEM((groups, height, lanes), F32),
            pltpu.VMEM((ny, height, lanes), F32),
            pltpu.VMEM((ny, height, lanes), F32),
            pltpu.VMEM((ny, height, lanes), F32),
            pltpu.VMEM((height, lanes), F32),
            pltpu.VMEM((nx, piece * nz, lanes), F32),
            pltpu.VMEM((nz, piece, lanes), F32),
            pltpu.VMEM((nz, piece, lanes), F32),
        ] + [dma(shape) for shape in sems],
        compiler_params=pltpu.CompilerParams(
            collective_id=0, has_side_effects=True, vmem_limit_bytes=60 << 20
        ),
        name="exchange",
    )(slot_orbital, domain_len, domain_blocks, occ_energy, table, pair_ints)


def project_kernel(
    slot_hbm, len_hbm, block_hbm, occ_hbm, packed_hbm, own_hbm, filter_ref, norm_ref, energy_hbm, out_hbm,
    packed_ref, own_ref, own_sem, slot_ref, len_ref, block_ref, occ_ref, small_sem, m_high, m_low, x_ref, r_ref, out_buf, energy_buf, out_sem, energy_sem,
):
    tiles, _, width = out_buf.shape
    blocks, _, side = energy_buf.shape
    def fetch(t):
        return pltpu.make_async_copy(own_hbm.at[t], own_ref.at[t], own_sem.at[t])

    for t in range(tiles):
        fetch(t).start()
    good = jnp.max(norm_ref[...]) < RESIDUAL_BOUND

    @pl.when(good)
    def _():
        m_high[...] = filter_ref[...]

    @pl.when(jnp.logical_not(good))
    def _():
        small = [(slot_hbm, slot_ref), (len_hbm, len_ref), (block_hbm, block_ref), (occ_hbm, occ_ref), (packed_hbm, packed_ref)]
        for k, (source, target) in enumerate(small):
            move = pltpu.make_async_copy(source, target, small_sem.at[k])
            move.start()
            move.wait()
        orbital = slot_ref[lax.axis_index("occ")]

        def energy(k):
            return pltpu.make_async_copy(
                energy_hbm.at[block_ref[orbital, k]], energy_buf.at[k], energy_sem.at[k]
            )

        for k in range(blocks):
            energy(k).start()
        for k in range(blocks):
            energy(k).wait()
        live = (side * len_ref[orbital]).astype(F32)
        start = prepare(
            lambda k: energy_buf[k], blocks, occ_ref[orbital], live, packed_ref, m_high, m_low, x_ref
        )
        m_high[...] = invert_checked(start, m_high, m_low, x_ref, r_ref).astype(BF16)

    def flush(t):
        return pltpu.make_async_copy(
            out_buf.at[t], out_hbm.at[:, pl.ds(t * width, width)], out_sem.at[t]
        )

    for t in range(tiles):
        fetch(t).wait()
        out_buf[t] = dot(m_high[...], own_ref[t]).astype(BF16)
        flush(t).start()
    for t in range(tiles):
        flush(t).wait()


def project(slot_orbital, domain_len, domain_blocks, occ_energy, packed, own, projector, norm, table):
    groups, size, width = own.shape
    blocks = domain_blocks.shape[1]
    side = size // blocks
    vmem = pl.BlockSpec(memory_space=pltpu.VMEM)
    hbm = pl.BlockSpec(memory_space=pltpu.HBM)
    return pl.pallas_call(
        project_kernel,
        out_shape=jax.ShapeDtypeStruct((size, groups * width), BF16),
        in_specs=[hbm] * 6 + [vmem] * 2 + [hbm],
        out_specs=pl.BlockSpec(memory_space=pl.ANY),
        scratch_shapes=[
            pltpu.VMEM(packed.shape, F32),
            pltpu.VMEM(own.shape, BF16),
            pltpu.SemaphoreType.DMA((groups,)),
            pltpu.SMEM(slot_orbital.shape, jnp.int32),
            pltpu.SMEM(domain_len.shape, jnp.int32),
            pltpu.SMEM(domain_blocks.shape, jnp.int32),
            pltpu.SMEM(occ_energy.shape, F32),
            pltpu.SemaphoreType.DMA((5,)),
            pltpu.VMEM((size, size), BF16),
            pltpu.VMEM((size, size), BF16),
            pltpu.VMEM((size, size), F32),
            pltpu.VMEM((size, size), F32),
            pltpu.VMEM((groups, size, width), BF16),
            pltpu.VMEM((blocks, 1, side), F32),
            pltpu.SemaphoreType.DMA((groups,)),
            pltpu.SemaphoreType.DMA((blocks,)),
        ],
        compiler_params=pltpu.CompilerParams(vmem_limit_bytes=60 << 20),
        name="project",
    )(slot_orbital, domain_len, domain_blocks, occ_energy, packed, own, projector, norm, table)


def solution(mesh):
    n_aux = mesh.shape["aux"]

    def local(pair_ints, domain_len, domain_blocks, slot_orbital, virt_energy, occ_energy):
        table = virt_energy.reshape(-1, 1, pair_ints.shape[1])
        gram, own, projector, norm = exchange(
            slot_orbital, domain_len, domain_blocks, occ_energy, table, pair_ints, n_aux
        )
        return project(
            slot_orbital, domain_len, domain_blocks, occ_energy, gram, own, projector, norm, table
        )[None]

    placed = (P(None, None, ("aux", "occ")), P(), P(), P(), P(), P())
    return jax.shard_map(
        local, mesh=mesh, in_specs=placed, out_specs=P("occ", None, "aux"), check_vma=False
    )
```
